128 devices in a mesh: gx: 8 (over x_hi, y), gy: 16 (over x_lo, z, core).
Axes of the slice: x: 4 (x_hi: 2, x_lo: 2; x = x_hi * 2 + x_lo), y: 4, z: 4, core: 2. Of those that a mesh axis runs over, the one named last changes fastest.
Arguments:
- features: bfloat16 [32, 128, 128, 128], P('gx', 'gy'), may hold values from -6 to 6
- positions: bfloat16 [32, 128, 3, 128], P('gx', 'gy'), may hold values from 0 to 1
- neighbours: int32 [32, 128, 4], P('gx', 'gy'), may hold values from 0 to 8, as said below
- atom_counts: int32 [32, 128], P('gx', 'gy'), may hold values from 64 to 128
- radial_bins: int32 [32, 128, 4, 128], P('gx', 'gy'), may hold values from 0 to 31
- destination: int32 [32, 128], P('gx', 'gy'), may hold values from 0 to 4095, as said below
- anchor: int32 [4096], P(('gx', 'gy')), may hold values from 0 to 4095, as said below
- weights: bfloat16 [32, 128, 128], replicated, may hold values from -0.09375 to 0.09375
- cotangent: bfloat16 [4096, 128, 128], P(('gx', 'gy')), may hold values from -6 to 6
Outputs:
- updated: bfloat16 [4096, 128, 128], P(('gx', 'gy'))
- feature_grad: bfloat16 [32, 128, 128, 128], P('gx', 'gy')
- weight_grad: float32 [4096, 128], P(('gx', 'gy'))
The draws below stay inside these ranges and needn't reach their ends.
Inputs may be any that keep to these rules, and one draw needn't show every extreme that they name: `neighbours`: entry 0 of every list is 4, the leaf itself; the other 3 entries are distinct codes 3 (dx + 1) + (dy + 1) of surrounding leaves at grid offset (dx, dy), dx and dy in -1, 0, 1, never 4. `destination`: one to one onto all 4096 owner slots; slot g belongs to device g // 32, devices numbered over gx then gy. Of one device's 32 leaves at most 1 goes to any one device, so each device sends its leaves to 32 distinct devices; and each device receives exactly 32 leaves, one from each of 32 distinct devices. The inverse of destination: anchor[destination[X, Y]] is the home id of leaf (X, Y).
All inputs are finite; a program needn't handle non-finite values.
Results may differ from the reference program's by a relative error of at most 0.0069.
Values may be sent and summed in bfloat16 or wider, within the bound.
No kernel may reach another device: no remote copies, remote signals or barrier semaphores. Data moves between devices by JAX's collectives and lax.ppermute only.
A program may use at most 128 MiB of HBM per device.

```python
import math
import jax
import jax.numpy as jnp
from jax import lax

LEAF_ATOM_SLOTS = 128
FEATURE_CHANNELS = 128
RADIAL = 32
NEIGH = 4
LX = 4
LY = 8
CAP = 1
NXL = 32
NYL = 128
LEAF_SLOT_TOTAL = 4096
N_GX = 8
N_GY = 16


def distinct_order(key, row_count, length):
    scores = jax.random.randint(key, (row_count, length), 0, 1 << 20, dtype=jnp.int32) * length
    scores = scores + jnp.arange(length, dtype=jnp.int32)[None, :]
    return jnp.argsort(scores, axis=1).astype(jnp.int32)


def plan_tables(key):
    base_key = jax.random.fold_in(key, 7)
    key_items, key_spread, key_target, key_start, key_landing = jax.random.split(base_key, 5)
    devices = N_GX * N_GY
    leaves = LX * LY
    slot_count = devices * CAP
    shuffled = jax.random.permutation(key_items, slot_count).astype(jnp.int32)
    ranking = jnp.argsort(shuffled).astype(jnp.int32)
    groups = jnp.arange(slot_count, dtype=jnp.int32) // CAP
    chosen = shuffled[0] // CAP
    scores = jnp.where(groups == chosen, -1, ranking)
    picked = jnp.argsort(scores)[:leaves].astype(jnp.int32)
    offsets = (picked // CAP).astype(jnp.int32)
    spread = distinct_order(key_spread, devices, leaves)
    target_slot = jax.random.permutation(key_target, devices).astype(jnp.int32)
    offset_start = jax.random.permutation(key_start, devices).astype(jnp.int32)
    landing = distinct_order(key_landing, devices, leaves)
    owner_device = target_slot[(offset_start[:, None] + offsets[spread]) % devices]
    landing_slot = landing[owner_device, spread]
    return (owner_device * leaves + landing_slot).astype(jnp.int32)


def draw_destination(key, part):
    global_slots = plan_tables(key)
    shaped = global_slots.reshape(N_GX, N_GY, LX, LY)
    return jnp.transpose(shaped, (0, 2, 1, 3)).reshape(NXL, NYL).astype(jnp.int32)


def draw_anchor(key, part):
    global_slots = plan_tables(key)
    return jnp.argsort(global_slots.reshape(-1)).astype(jnp.int32)


def draw_neighbours(key, part):
    ranking = distinct_order(jax.random.fold_in(key, 11), NXL * NYL, 8)
    chosen = ranking[:, :NEIGH - 1]
    code_list = jnp.where(chosen >= 4, chosen + 1, chosen)
    itself = jnp.full((NXL * NYL, 1), 4, jnp.int32)
    return jnp.concatenate([itself, code_list], axis=1).reshape(NXL, NYL, NEIGH).astype(jnp.int32)


def set_ends(result, own_key, low, high):
    longest = result.shape.index(max(result.shape))
    spots = []
    for shift in (0, 1):
        where = [jax.random.randint(jax.random.fold_in(own_key, axis), (), 0, length) for axis, length in enumerate(result.shape)]
        where[longest] = (where[longest] + shift) % result.shape[longest]
        spots.append(tuple(where))
    return result.at[spots[0]].set(low).at[spots[1]].set(high)


def levels(stream_key, dims, cuts, smallest, largest):
    gain = 1.0
    for axis_at, blocks in cuts:
        draws = jax.random.uniform(jax.random.fold_in(jax.random.fold_in(stream_key, 6), axis_at), (blocks,), jnp.float32, smallest / len(cuts), largest / len(cuts))
        gain = gain * jnp.repeat(jnp.exp(draws), dims[axis_at] // blocks).reshape((-1,) + (1,) * (len(dims) - 1 - axis_at))
    return gain


def centred(stream_key, extent, scale, reach, shards=(), kind=jnp.bfloat16):
    gain = levels(stream_key, extent, shards, -0.22, 0.18) if shards else 1.0
    values = jax.random.normal(stream_key, extent, jnp.float32) * scale * gain
    return jnp.minimum(jnp.maximum(values, -reach), reach).astype(kind)


def setup_inputs(seed: int = 0) -> dict:
    arg_keys = jax.random.split(jax.random.key(seed), 10)
    return {
        "features": centred(arg_keys[0], (NXL, NYL, LEAF_ATOM_SLOTS, FEATURE_CHANNELS), 1.0, 6.0, ((0, 8), (1, 16))),
        "positions": jnp.clip(1.0 * jax.random.uniform(arg_keys[1], (NXL, NYL, 3, LEAF_ATOM_SLOTS), jnp.float32) ** levels(arg_keys[1], (NXL, NYL, 3, LEAF_ATOM_SLOTS), ((0, 8), (1, 16)), -0.2, 0.2), 0.0, 1.0).astype(jnp.bfloat16),
        "neighbours": draw_neighbours(jax.random.fold_in(arg_keys[9], 71), 0),
        "atom_counts": set_ends(jax.random.randint(arg_keys[3], (NXL, NYL), LEAF_ATOM_SLOTS // 2, LEAF_ATOM_SLOTS + 1), jax.random.fold_in(arg_keys[3], 1), LEAF_ATOM_SLOTS // 2, LEAF_ATOM_SLOTS).astype(jnp.int32),
        "radial_bins": set_ends(jax.random.randint(arg_keys[4], (NXL, NYL, NEIGH, LEAF_ATOM_SLOTS), 0, RADIAL), jax.random.fold_in(arg_keys[4], 1), 0, RADIAL - 1).astype(jnp.int32),
        "destination": draw_destination(jax.random.fold_in(arg_keys[9], 71), 0),
        "anchor": draw_anchor(jax.random.fold_in(arg_keys[9], 71), 0),
        "weights": centred(arg_keys[7], (RADIAL, FEATURE_CHANNELS, FEATURE_CHANNELS), (RADIAL * FEATURE_CHANNELS) ** -0.5, 0.09375),
        "cotangent": centred(arg_keys[8], (LEAF_SLOT_TOTAL, LEAF_ATOM_SLOTS, FEATURE_CHANNELS), 1.0, 6.0, ((0, 128),)),
    }


SHARPNESS = 2.0

def pairwise_coupling(receiver, sender_xyz, offset_codes):
    receiving = receiver.astype(jnp.float32)
    remote = sender_xyz.astype(jnp.float32)
    shift_x = (offset_codes // 3 - 1).astype(jnp.float32)
    shift_y = (offset_codes % 3 - 1).astype(jnp.float32)
    delta_x = remote[:, :, 0, None, :] + shift_x[:, :, None, None] - receiving[:, None, 0, :, None]
    delta_y = remote[:, :, 1, None, :] + shift_y[:, :, None, None] - receiving[:, None, 1, :, None]
    delta_z = remote[:, :, 2, None, :] - receiving[:, None, 2, :, None]
    distance = delta_x * delta_x + delta_y * delta_y + delta_z * delta_z
    slot_count = receiving.shape[-1]
    row_index = lax.broadcasted_iota(jnp.int32, (slot_count, slot_count), 0)
    col_index = lax.broadcasted_iota(jnp.int32, (slot_count, slot_count), 1)
    itself = (offset_codes == 4)[:, :, None, None] & (row_index == col_index)[None, None]
    return jnp.where(itself, 0.0, jnp.exp(-SHARPNESS * distance)).astype(jnp.bfloat16)

def leaf_order(array, grid_rows, grid_cols):
    tail = array.shape[2:]
    shaped = array.reshape((N_GX, grid_rows, N_GY, grid_cols) + tail)
    return jnp.moveaxis(shaped, 2, 1).reshape((N_GX * N_GY * grid_rows * grid_cols,) + tail)

def grid_order(array, grid_rows, grid_cols):
    tail = array.shape[1:]
    shaped = array.reshape((N_GX, N_GY, grid_rows, grid_cols) + tail)
    return jnp.moveaxis(shaped, 1, 2).reshape((N_GX * grid_rows, N_GY * grid_cols) + tail)

def reference(features, positions, neighbours, atom_counts, radial_bins, destination, anchor, weights, cotangent):
    total_rows, total_cols, slot_count, channel_count = features.shape
    grid_rows = total_rows // N_GX
    grid_cols = total_cols // N_GY
    leaves = grid_rows * grid_cols
    total = leaves * N_GX * N_GY
    radial = weights.shape[0]
    home_ids = jnp.arange(total, dtype=jnp.int32)
    device_of = home_ids // leaves
    within = home_ids % leaves
    row_of = device_of // N_GY * grid_rows + within // grid_cols
    col_of = device_of % N_GY * grid_cols + within % grid_cols
    offset_codes = leaf_order(neighbours, grid_rows, grid_cols)
    sender_row = (row_of[:, None] + offset_codes // 3 - 1) % total_rows
    sender_col = (col_of[:, None] + offset_codes % 3 - 1) % total_cols
    sender_home = ((sender_row // grid_rows * N_GY + sender_col // grid_cols) * leaves + sender_row % grid_rows * grid_cols + sender_col % grid_cols).astype(jnp.int32)
    counts_ordered = leaf_order(atom_counts, grid_rows, grid_cols)
    valid = (jnp.arange(slot_count, dtype=jnp.int32)[None, :] < counts_ordered[:, None]).astype(jnp.float32)
    masked = leaf_order(features, grid_rows, grid_cols) * valid[:, :, None].astype(jnp.bfloat16)
    located = leaf_order(positions, grid_rows, grid_cols)
    bin_order = leaf_order(radial_bins, grid_rows, grid_cols)
    home_grad = cotangent[leaf_order(destination, grid_rows, grid_cols).astype(jnp.int32)]
    weight_rows = weights.reshape(radial * channel_count, channel_count).astype(jnp.float32)
    block_size = math.gcd(total, 32)
    highest = lax.Precision.HIGHEST

    def leaf_step(carry, first_leaf):
        grad_total, weight_total = carry
        members = (first_leaf + jnp.arange(block_size, dtype=jnp.int32)).astype(jnp.int32)
        sender_ids = sender_home[members]
        coupling = pairwise_coupling(located[members], located[sender_ids], offset_codes[members]).astype(jnp.float32)
        tile_sums = jnp.einsum('bnij,bnjc->bnic', coupling, masked[sender_ids].astype(jnp.float32), precision=highest)
        selection_mask = (bin_order[members][..., None] == jnp.arange(radial, dtype=jnp.int32)).astype(jnp.float32)
        gathered = jnp.einsum('bnik,bnic->bikc', selection_mask, tile_sums, precision=highest).astype(jnp.bfloat16)
        flat_rows = gathered.reshape(block_size * slot_count, radial * channel_count).astype(jnp.float32)
        message = jnp.dot(flat_rows, weight_rows, precision=highest, preferred_element_type=jnp.float32)
        valid_col = valid[members].reshape(-1, 1)
        outgoing = (jax.nn.silu(message) * valid_col).astype(jnp.bfloat16)
        logistic = jax.nn.sigmoid(message)
        gradient_slope = logistic * (1.0 + message * (1.0 - logistic))
        message_grad = (home_grad[members].reshape(-1, channel_count).astype(jnp.float32) * valid_col * gradient_slope).astype(jnp.bfloat16)
        gradient_rows = message_grad.astype(jnp.float32)
        full_grad = jnp.dot(gradient_rows, weight_rows.T, precision=highest, preferred_element_type=jnp.float32).astype(jnp.bfloat16)
        full_grad = full_grad.reshape(block_size, slot_count, radial, channel_count).astype(jnp.float32)
        tile_grad = jnp.einsum('bnik,bikc->bnic', selection_mask, full_grad, precision=highest).astype(jnp.bfloat16)
        sender_grad = jnp.einsum('bnij,bnic->bnjc', coupling, tile_grad.astype(jnp.float32), precision=highest)
        grad_total = grad_total.at[sender_ids.reshape(-1)].add(sender_grad.reshape(-1, slot_count, channel_count))
        weight_total = weight_total + jnp.dot(flat_rows.T, gradient_rows, precision=highest, preferred_element_type=jnp.float32)
        return ((grad_total, weight_total), outgoing.reshape(block_size, slot_count, channel_count))
    first_leaves = jnp.arange(0, total, block_size, dtype=jnp.int32)
    initial = (jnp.zeros((total, slot_count, channel_count), jnp.float32), jnp.zeros((radial * channel_count, channel_count), jnp.float32))
    (grad_total, weight_total), outputs = lax.scan(leaf_step, initial, first_leaves)
    home_out = outputs.reshape(total, slot_count, channel_count)
    updated = home_out[anchor.astype(jnp.int32)]
    feature_grad = grid_order((grad_total * valid[:, :, None]).astype(jnp.bfloat16), grid_rows, grid_cols)
    weight_grad = weight_total * (1.0 / math.sqrt(total * slot_count))
    return (updated, feature_grad, weight_grad)
```

```python
import functools
import math

import jax
import jax.numpy as jnp
from jax import lax
from jax.experimental import pallas as pl
from jax.experimental.pallas import tpu as pltpu
from jax.sharding import PartitionSpec as P


AXES = ("gx", "gy")
SHARPNESS = 2.0
FAR = 9984.0
POS_ROWS = 16
BLOCK = 4
VMEM_LIMIT = 60 * 1024 * 1024

f32 = jnp.float32
bf16 = jnp.bfloat16

STEPS = ((1, 0), (-1, 0), (0, 1), (0, -1), (1, 1), (1, -1), (-1, 1), (-1, -1))


def picks(step, grid, low, span):
    if step == 0:
        return list(range(low, low + span))
    return [grid[1]] if step > 0 else [grid[0]]


def border(step, rows, cols):
    return [
        (r, c)
        for r in picks(step[0], (0, rows - 1), 0, rows)
        for c in picks(step[1], (0, cols - 1), 0, cols)
    ]


def rim(step, rows, cols):
    return [
        (r, c)
        for r in picks(step[0], (0, rows + 1), 1, rows)
        for c in picks(step[1], (0, cols + 1), 1, cols)
    ]


def vmem(*_):
    return pl.BlockSpec(memory_space=pltpu.VMEM)


def hbm(*_):
    return pl.BlockSpec(memory_space=pl.ANY)


def smem(*_):
    return pl.BlockSpec(memory_space=pltpu.SMEM)


def params(**extra):
    return pltpu.CompilerParams(vmem_limit_bytes=VMEM_LIMIT, **extra)


def pack_kernel(dims, counts, slots, features, positions, cotangent, *rest):
    rows, cols, slot_count = dims
    leaves = rows * cols
    home, *sends = rest[:9]
    packed, sem = rest[9:]
    copies = [
        pltpu.make_async_copy(cotangent.at[g], packed.at[slots[g]], sem.at[g])
        for g in range(leaves)
    ]
    for copy in copies:
        copy.start()
    lane = lax.broadcasted_iota(jnp.int32, (1, slot_count), 1)
    pad = jnp.zeros((POS_ROWS - 3, slot_count), f32)
    for r in range(rows):
        place = [positions[r, axis].astype(f32) for axis in range(3)]
        for c in range(cols):
            leaf = r * cols + c
            x = jnp.where(lane < counts[leaf], place[0][c : c + 1], FAR)
            block = jnp.concatenate([x, place[1][c : c + 1], place[2][c : c + 1], pad], axis=0)
            home[leaf, slot_count:, :] = block.astype(bf16)
    home[:, :slot_count, :] = features[...]
    for step, send in zip(STEPS, sends):
        for index, (r, c) in enumerate(border(step, rows, cols)):
            send[index] = home[r * cols + c]
    for copy in copies:
        copy.wait()


def leaf_columns(place, bins):
    return jnp.concatenate([place, bins.astype(f32)], axis=0).T


def forward_kernel(dims, codes, counts, slots, home, *rest):
    rows, cols, slot_count, channels, radial, neigh = dims
    halos = rest[:8]
    bins_ref, weights = rest[8:10]
    gathered, slope, coupling_out, packed = rest[10:14]
    ghost, message, outgoing, sem_in, sem_out = rest[14:]
    block = pl.program_id(0)
    wide = cols + 2

    @pl.when(block == 0)
    def _():
        copies = []
        for r in range(rows):
            copies.append((home.at[pl.ds(r * cols, cols)], ghost.at[pl.ds((r + 1) * wide + 1, cols)]))
        for step, halo in zip(STEPS, halos):
            spots = rim((-step[0], -step[1]), rows, cols)
            if step[1] == 0:
                first = spots[0][0] * wide + spots[0][1]
                copies.append((halo, ghost.at[pl.ds(first, cols)]))
            else:
                for index, (r, c) in enumerate(spots):
                    copies.append((halo.at[index], ghost.at[r * wide + c]))
        copies = [
            pltpu.make_async_copy(source, target, sem_in.at[index])
            for index, (source, target) in enumerate(copies)
        ]
        for copy in copies:
            copy.start()
        for copy in copies:
            copy.wait()

    row_index = lax.broadcasted_iota(jnp.int32, (slot_count, slot_count), 0)
    col_index = lax.broadcasted_iota(jnp.int32, (slot_count, slot_count), 1)

    def leaf_step(index, carry):
        leaf = block * BLOCK + index
        r = leaf // cols
        c = leaf % cols
        own = (r + 1) * wide + c + 1
        place = ghost[own, pl.ds(slot_count, POS_ROWS), :].astype(f32)
        columns = leaf_columns(place[:4], bins_ref[leaf])
        receiver = [
            jnp.broadcast_to(columns[:, axis : axis + 1], (slot_count, slot_count))
            for axis in range(3)
        ]
        bins = [
            jnp.broadcast_to(columns[:, 4 + n : 5 + n], (slot_count, channels))
            for n in range(neigh)
        ]
        tiles = []
        for n in range(neigh):
            code = codes[leaf * neigh + n]
            row_off = code // 3
            col_off = code % 3
            sender = (r + row_off) * wide + c + col_off
            remote = ghost[sender, pl.ds(slot_count, POS_ROWS), :].astype(f32)
            delta_x = (remote[0:1] + (row_off - 1).astype(f32)) - receiver[0]
            delta_y = (remote[1:2] + (col_off - 1).astype(f32)) - receiver[1]
            delta_z = remote[2:3] - receiver[2]
            distance = delta_x * delta_x + delta_y * delta_y + delta_z * delta_z
            coupling = jnp.exp(-SHARPNESS * distance)
            if n == 0:
                coupling = jnp.where(row_index == col_index, 0.0, coupling)
            coupling = coupling.astype(bf16)
            coupling_out[index * neigh + n] = coupling
            tiles.append(
                jnp.dot(coupling, ghost[sender, pl.ds(0, slot_count), :], preferred_element_type=f32)
            )
        merged = []
        for n in range(neigh):
            total = tiles[n]
            for m in range(n):
                total = total + jnp.where(bins[m] == bins[n], tiles[m], 0.0)
            merged.append(total.astype(bf16))
        marks = [value.astype(bf16) for value in bins]
        base = pl.multiple_of(index * slot_count, slot_count)
        for k in range(radial):
            value = jnp.zeros((slot_count, channels), bf16)
            for n in range(neigh):
                value = jnp.where(marks[n] == jnp.bfloat16(k), merged[n], value)
            gathered[pl.ds(base, slot_count), k * channels : (k + 1) * channels] = value
        return carry

    lax.fori_loop(0, BLOCK, leaf_step, 0)
    message[...] = jnp.dot(gathered[...], weights[...], preferred_element_type=f32)

    def sends(at):
        return [
            pltpu.make_async_copy(
                outgoing.at[index], packed.at[slots[at * BLOCK + index]], sem_out.at[index]
            )
            for index in range(BLOCK)
        ]

    @pl.when(block > 0)
    def _():
        for copy in sends(block - 1):
            copy.wait()

    for index in range(BLOCK):
        value = message[index * slot_count : (index + 1) * slot_count]
        valid = (row_index < counts[block * BLOCK + index]).astype(f32)
        logistic = 1.0 / (1.0 + jnp.exp(-value))
        outgoing[index] = (value * logistic * valid).astype(bf16)
        slope[index * slot_count : (index + 1) * slot_count] = (
            valid * logistic * (1.0 + value * (1.0 - logistic))
        )
    for copy in sends(block):
        copy.start()

    @pl.when(block == pl.num_programs(0) - 1)
    def _():
        for copy in sends(block):
            copy.wait()


def weight_kernel(dims, slots, gathered, slope, returned, mg_out, grad, home_grad, total, sem):
    leaves, slot_count, channels, radial = dims
    block = pl.program_id(0)

    @pl.when(block == 0)
    def _():
        copies = [
            pltpu.make_async_copy(returned.at[slots[leaf]], home_grad.at[leaf], sem.at[leaf])
            for leaf in range(leaves)
        ]
        for copy in copies:
            copy.start()
        for copy in copies:
            copy.wait()
        total[...] = jnp.zeros_like(total)

    incoming = home_grad[pl.ds(block * BLOCK, BLOCK)].reshape(BLOCK * slot_count, channels)
    message_grad = (incoming.astype(f32) * slope[...]).astype(bf16)
    mg_out[...] = message_grad
    total[...] += lax.dot_general(
        message_grad, gathered[...], (((0,), (0,)), ((), ())), preferred_element_type=f32
    )

    @pl.when(block == pl.num_programs(0) - 1)
    def _():
        for k in range(radial):
            grad[k * channels : (k + 1) * channels, :] = (
                total[:, k * channels : (k + 1) * channels].T.astype(grad.dtype)
            )


def backward_kernel(dims, codes, mg, coupling, bins_ref, weights, *rest):
    rows, cols, slot_count, channels, radial, neigh = dims
    own = rest[0]
    sends = rest[1:9]
    padded, full = rest[9:]
    block = pl.program_id(0)
    wide = cols + 2

    @pl.when(block == 0)
    def _():
        padded[...] = jnp.zeros_like(padded)

    full[...] = lax.dot_general(
        mg[...], weights[...], (((1,), (1,)), ((), ())), preferred_element_type=f32
    ).astype(bf16)
    half = slot_count // 2

    def leaf_step(index, carry):
        leaf = block * BLOCK + index
        r = leaf // cols
        c = leaf % cols
        columns = leaf_columns(jnp.zeros((4, slot_count), f32), bins_ref[leaf])
        marks = [
            jnp.broadcast_to(columns[:, 4 + n : 5 + n], (slot_count, channels)).astype(bf16)
            for n in range(neigh)
        ]
        parts = [[] for _ in range(neigh)]
        for part in range(2):
            base = pl.multiple_of(index * slot_count + part * half, half)
            values = [jnp.zeros((half, channels), bf16)] * neigh
            for k in range(radial):
                row = full[pl.ds(base, half), k * channels : (k + 1) * channels]
                for n in range(neigh):
                    mark = marks[n][part * half : (part + 1) * half]
                    values[n] = jnp.where(mark == jnp.bfloat16(k), row, values[n])
            for n in range(neigh):
                parts[n].append(values[n])
        for n in range(neigh):
            tile_grad = jnp.concatenate(parts[n], axis=0)
            code = codes[leaf * neigh + n]
            sender = (r + code // 3) * wide + c + code % 3
            padded[sender] += lax.dot_general(
                coupling[index * neigh + n],
                tile_grad,
                (((0,), (0,)), ((), ())),
                preferred_element_type=f32,
            )
        return carry

    lax.fori_loop(0, BLOCK, leaf_step, 0)

    @pl.when(block == pl.num_programs(0) - 1)
    def _():
        for r in range(rows):
            first = (r + 1) * wide + 1
            own[r * cols : (r + 1) * cols] = padded[first : first + cols]
        for step, send in zip(STEPS, sends):
            for index, (r, c) in enumerate(rim(step, rows, cols)):
                send[index] = padded[r * wide + c].astype(send.dtype)


def fold_kernel(dims, own, *rest):
    rows, cols = dims
    received = rest[:8]
    out, total = rest[8:]
    total[...] = own[...]
    for step, piece in zip(STEPS, received):
        for index, (r, c) in enumerate(border((-step[0], -step[1]), rows, cols)):
            total[r * cols + c] += piece[index].astype(f32)
    out[...] = total[...].astype(bf16)


def collect_kernel(leaves, slots, arrived, out, sem):
    copies = [
        pltpu.make_async_copy(arrived.at[slots[g]], out.at[g], sem.at[g]) for g in range(leaves)
    ]
    for copy in copies:
        copy.start()
    for copy in copies:
        copy.wait()


def shift(value, step, shape):
    gx, gy = shape
    pairs = [
        (i * gy + j, (i + step[0]) % gx * gy + (j + step[1]) % gy)
        for i in range(gx)
        for j in range(gy)
    ]
    return lax.ppermute(value, AXES, pairs)


def relay(buffer):
    return lax.all_to_all(buffer, AXES, split_axis=0, concat_axis=0, tiled=True)


def shards(
    features,
    positions,
    neighbours,
    atom_counts,
    radial_bins,
    destination,
    anchor,
    weights,
    cotangent,
):
    rows, cols, slot_count, channels = features.shape
    neigh = neighbours.shape[2]
    radial = weights.shape[0]
    leaves = rows * cols
    shape = (lax.axis_size("gx"), lax.axis_size("gy"))
    peers = shape[0] * shape[1]
    padded = (rows + 2) * (cols + 2)
    blocks = leaves // BLOCK
    tall = slot_count + POS_ROWS
    width = radial * channels
    any_dma = pltpu.SemaphoreType.DMA

    counts = atom_counts.reshape(leaves)
    codes = neighbours.reshape(leaves * neigh)
    home_slots = destination.reshape(leaves) // leaves
    owner_slots = anchor // leaves
    bins = radial_bins.reshape(leaves, neigh, slot_count)
    weight_rows = weights.reshape(width, channels)
    sizes = [len(border(step, rows, cols)) for step in STEPS]

    home, *rest = pl.pallas_call(
        functools.partial(pack_kernel, (rows, cols, slot_count)),
        out_shape=[jax.ShapeDtypeStruct((leaves, tall, channels), bf16)]
        + [jax.ShapeDtypeStruct((size, tall, channels), bf16) for size in sizes]
        + [jax.ShapeDtypeStruct((peers, slot_count, channels), bf16)],
        in_specs=[smem(), smem(), vmem(), vmem(), vmem()],
        out_specs=[vmem()] * 9 + [hbm()],
        scratch_shapes=[any_dma((leaves,))],
        compiler_params=params(),
        name="pack",
    )(
        counts,
        owner_slots,
        features.reshape(leaves, slot_count, channels),
        positions.transpose(0, 2, 1, 3),
        cotangent,
    )
    sends, cot_packed = rest[:8], rest[8]
    halos = []
    for send, step in zip(sends, STEPS):
        halos.append(shift(send, step, shape))
    returned = relay(cot_packed)

    gathered, slope, coupling, packed = pl.pallas_call(
        functools.partial(forward_kernel, (rows, cols, slot_count, channels, radial, neigh)),
        grid=(blocks,),
        out_shape=[
            jax.ShapeDtypeStruct((leaves * slot_count, width), bf16),
            jax.ShapeDtypeStruct((leaves * slot_count, channels), f32),
            jax.ShapeDtypeStruct((leaves * neigh, slot_count, slot_count), bf16),
            jax.ShapeDtypeStruct((peers, slot_count, channels), bf16),
        ],
        in_specs=[smem(), smem(), smem(), hbm()] + [hbm()] * 8 + [vmem(), vmem()],
        out_specs=[
            pl.BlockSpec((BLOCK * slot_count, width), lambda b: (b, 0)),
            pl.BlockSpec((BLOCK * slot_count, channels), lambda b: (b, 0)),
            pl.BlockSpec((BLOCK * neigh, slot_count, slot_count), lambda b: (b, 0, 0)),
            hbm(),
        ],
        scratch_shapes=[
            pltpu.VMEM((padded, tall, channels), bf16),
            pltpu.VMEM((BLOCK * slot_count, channels), f32),
            pltpu.VMEM((BLOCK, slot_count, channels), bf16),
            any_dma((2 * (rows + cols) + rows + 8,)),
            any_dma((BLOCK,)),
        ],
        compiler_params=params(dimension_semantics=("arbitrary",)),
        name="forward",
    )(codes, counts, home_slots, home, *halos, bins, weight_rows)

    arrived = relay(packed)

    message_grad, weight_part = pl.pallas_call(
        functools.partial(weight_kernel, (leaves, slot_count, channels, radial)),
        grid=(blocks,),
        out_shape=[
            jax.ShapeDtypeStruct((leaves * slot_count, channels), bf16),
            jax.ShapeDtypeStruct((width, channels), bf16),
        ],
        in_specs=[
            smem(),
            pl.BlockSpec((BLOCK * slot_count, width), lambda b: (b, 0)),
            pl.BlockSpec((BLOCK * slot_count, channels), lambda b: (b, 0)),
            hbm(),
        ],
        out_specs=[
            pl.BlockSpec((BLOCK * slot_count, channels), lambda b: (b, 0)),
            pl.BlockSpec((width, channels), lambda b: (0, 0)),
        ],
        scratch_shapes=[
            pltpu.VMEM((leaves, slot_count, channels), bf16),
            pltpu.VMEM((channels, width), f32),
            any_dma((leaves,)),
        ],
        compiler_params=params(dimension_semantics=("arbitrary",)),
        name="weight",
    )(home_slots, gathered, slope, returned)

    weight_pieces = relay(weight_part.reshape(peers, width // peers, channels))

    own, *grad_sends = pl.pallas_call(
        functools.partial(backward_kernel, (rows, cols, slot_count, channels, radial, neigh)),
        grid=(blocks,),
        out_shape=[jax.ShapeDtypeStruct((leaves, slot_count, channels), f32)]
        + [jax.ShapeDtypeStruct((size, slot_count, channels), bf16) for size in sizes],
        in_specs=[
            smem(),
            pl.BlockSpec((BLOCK * slot_count, channels), lambda b: (b, 0)),
            pl.BlockSpec((BLOCK * neigh, slot_count, slot_count), lambda b: (b, 0, 0)),
            vmem(),
            vmem(),
        ],
        out_specs=[vmem()] * 9,
        scratch_shapes=[
            pltpu.VMEM((padded, slot_count, channels), f32),
            pltpu.VMEM((BLOCK * slot_count, width), bf16),
        ],
        compiler_params=params(dimension_semantics=("arbitrary",)),
        name="backward",
    )(codes, message_grad, coupling, bins, weight_rows)

    received = []
    for send, step in zip(grad_sends, STEPS):
        received.append(shift(send, step, shape))
    feature_grad = pl.pallas_call(
        functools.partial(fold_kernel, (rows, cols)),
        out_shape=jax.ShapeDtypeStruct((leaves, slot_count, channels), bf16),
        in_specs=[vmem()] * 9,
        out_specs=vmem(),
        scratch_shapes=[pltpu.VMEM((leaves, slot_count, channels), f32)],
        compiler_params=params(),
        name="fold",
    )(own, *received)

    updated = pl.pallas_call(
        functools.partial(collect_kernel, leaves),
        out_shape=jax.ShapeDtypeStruct((leaves, slot_count, channels), bf16),
        in_specs=[smem(), hbm()],
        out_specs=vmem(),
        scratch_shapes=[any_dma((leaves,))],
        compiler_params=params(),
        name="collect",
    )(owner_slots, arrived)

    grad_scale = 1.0 / math.sqrt(peers * leaves * slot_count)
    weight_grad = jnp.sum(weight_pieces.astype(f32), axis=0) * grad_scale
    return updated, feature_grad.reshape(rows, cols, slot_count, channels), weight_grad


def solution(mesh):
    leaf = P("gx", "gy")
    placed = (leaf, leaf, leaf, leaf, leaf, leaf, P(AXES), P(), P(AXES))
    return jax.shard_map(
        shards,
        mesh=mesh,
        in_specs=placed,
        out_specs=(P(AXES), leaf, P(AXES)),
        check_vma=False,
    )
```

```python
import functools
import math

import jax
import jax.numpy as jnp
from jax import lax
from jax.experimental import pallas as pl
from jax.experimental.pallas import tpu as pltpu
from jax.sharding import PartitionSpec as P


AXES = ("gx", "gy")
SHARPNESS = 2.0
FAR = 9984.0
POS_ROWS = 16
BLOCK = 4
TILE = 16
VMEM_LIMIT = 60 * 1024 * 1024

f32 = jnp.float32
bf16 = jnp.bfloat16

SIDES = 4
STEPS = ((1, 0), (-1, 0), (0, 1), (0, -1), (1, 1), (1, -1), (-1, 1), (-1, -1))


def picks(step, grid, low, span):
    if step == 0:
        return list(range(low, low + span))
    return [grid[1]] if step > 0 else [grid[0]]


def border(step, rows, cols):
    return [
        (r, c)
        for r in picks(step[0], (0, rows - 1), 0, rows)
        for c in picks(step[1], (0, cols - 1), 0, cols)
    ]


def rim(step, rows, cols):
    return [
        (r, c)
        for r in picks(step[0], (0, rows + 1), 1, rows)
        for c in picks(step[1], (0, cols + 1), 1, cols)
    ]


def vmem(*_):
    return pl.BlockSpec(memory_space=pltpu.VMEM)


def hbm(*_):
    return pl.BlockSpec(memory_space=pl.ANY)


def smem(*_):
    return pl.BlockSpec(memory_space=pltpu.SMEM)


def params(**extra):
    return pltpu.CompilerParams(vmem_limit_bytes=VMEM_LIMIT, **extra)


def pack_kernel(dims, counts, slots, features, positions, cotangent, *rest):
    rows, cols, slot_count = dims
    leaves = rows * cols
    home, *sends = rest[: SIDES + 1]
    packed, sem = rest[SIDES + 1 :]
    copies = [
        pltpu.make_async_copy(cotangent.at[g], packed.at[slots[g] // leaves], sem.at[g])
        for g in range(leaves)
    ]
    for copy in copies:
        copy.start()
    lane = lax.broadcasted_iota(jnp.int32, (1, slot_count), 1)
    pad = jnp.zeros((POS_ROWS - 3, slot_count), f32)
    for r in range(rows):
        place = [positions[r, axis].astype(f32) for axis in range(3)]
        for c in range(cols):
            leaf = r * cols + c
            x = jnp.where(lane < counts[r, c], place[0][c : c + 1], FAR)
            block = jnp.concatenate([x, place[1][c : c + 1], place[2][c : c + 1], pad], axis=0)
            home[leaf, slot_count:, :] = block.astype(bf16)
    home[:, :slot_count, :] = features[...]
    for step, send in zip(STEPS, sends):
        for index, (r, c) in enumerate(border(step, rows, cols)):
            send[index] = home[r * cols + c]
    for copy in copies:
        copy.wait()


def forward_kernel(dims, codes, counts, slots, home, *rest):
    rows, cols, slot_count, channels, radial, neigh = dims
    halos = rest[: SIDES + 2]
    bins_ref, weights = rest[SIDES + 2 : SIDES + 4]
    slope, coupling_out, gathered, packed = rest[SIDES + 4 : SIDES + 8]
    ghost, turned, weights_t, outgoing, sem_in, sem_out = rest[SIDES + 8 :]
    block = pl.program_id(0)
    wide = cols + 2
    leaves = rows * cols

    @pl.when(block == 0)
    def _():
        copies = []
        for r in range(rows):
            copies.append((home.at[pl.ds(r * cols, cols)], ghost.at[pl.ds((r + 1) * wide + 1, cols)]))
        spots = [rim((-step[0], -step[1]), rows, cols) for step in STEPS[:SIDES]]
        spots += [[(0, c), (rows + 1, c)] for c in (0, cols + 1)]
        for spot, halo in zip(spots, halos):
            if len(spot) == cols:
                copies.append((halo, ghost.at[pl.ds(spot[0][0] * wide + spot[0][1], cols)]))
            else:
                for index, (r, c) in enumerate(spot):
                    copies.append((halo.at[index], ghost.at[r * wide + c]))
        copies = [
            pltpu.make_async_copy(source, target, sem_in.at[index])
            for index, (source, target) in enumerate(copies)
        ]
        for copy in copies:
            copy.start()
        for k in range(radial):
            weights_t[:, k * channels : (k + 1) * channels] = weights[
                k * channels : (k + 1) * channels, :
            ].T
        for copy in copies:
            copy.wait()

        def turn(leaf, carry):
            turned[leaf] = ghost[leaf, pl.ds(0, slot_count), :].T
            return carry

        lax.fori_loop(0, (rows + 2) * wide, turn, 0, unroll=4)

    row_index = lax.broadcasted_iota(jnp.int32, (slot_count, slot_count), 0)
    col_index = lax.broadcasted_iota(jnp.int32, (slot_count, slot_count), 1)
    lane = lax.broadcasted_iota(jnp.int32, (channels, slot_count), 1)

    def place_of(leaf):
        return leaf // cols, leaf % cols

    def build(index):
        leaf = block * BLOCK + index
        r, c = place_of(leaf)
        own = (r + 1) * wide + c + 1
        place = ghost[own, pl.ds(slot_count, POS_ROWS), :].astype(f32)
        columns = place[:8].T
        receiver = [
            jnp.broadcast_to(columns[:, axis : axis + 1], (slot_count, slot_count))
            for axis in range(3)
        ]
        bins = bins_ref[leaf]
        tiles = []
        for n in range(neigh):
            code = codes[r, n, c]
            row_off = code // 3
            col_off = code % 3
            sender = (r + row_off) * wide + c + col_off
            remote = ghost[sender, pl.ds(slot_count, POS_ROWS), :].astype(f32)
            delta_x = (remote[0:1] + (row_off - 1).astype(f32)) - receiver[0]
            delta_y = (remote[1:2] + (col_off - 1).astype(f32)) - receiver[1]
            delta_z = remote[2:3] - receiver[2]
            distance = delta_x * delta_x + delta_y * delta_y + delta_z * delta_z
            coupling = jnp.exp(-SHARPNESS * distance)
            if n == 0:
                coupling = jnp.where(row_index == col_index, 0.0, coupling)
            coupling = coupling.astype(bf16)
            coupling_out[index * neigh + n] = coupling
            tiles.append(
                lax.dot_general(
                    turned[sender],
                    coupling,
                    (((1,), (1,)), ((), ())),
                    preferred_element_type=f32,
                )
            )
        merged = []
        for n in range(neigh):
            total = tiles[n]
            for m in range(n):
                same = jnp.broadcast_to(bins[m : m + 1] == bins[n : n + 1], total.shape)
                total = total + jnp.where(same, tiles[m], 0.0)
            merged.append(total.astype(bf16))
        marks = bin_marks(bins)
        for k in range(radial):
            masks = [mark == jnp.bfloat16(k) for mark in marks]
            for part in range(channels // TILE):
                value = jnp.zeros((TILE, slot_count), bf16)
                for n in range(neigh):
                    value = jnp.where(
                        masks[n], merged[n][part * TILE : (part + 1) * TILE], value
                    )
                first = k * channels + part * TILE
                gathered[index, first : first + TILE, :] = value

    def sends(at):
        copies = []
        for index in range(BLOCK):
            r, c = place_of(at * BLOCK + index)
            copies.append(
                pltpu.make_async_copy(
                    outgoing.at[index], packed.at[slots[r, c] // leaves], sem_out.at[index]
                )
            )
        return copies

    @pl.when(block > 0)
    def _():
        for copy in sends(block - 1):
            copy.wait()

    for pair in range(BLOCK // 2):
        for index in (2 * pair, 2 * pair + 1):
            build(index)
        message = jnp.dot(
            weights_t[...],
            jnp.concatenate([gathered[2 * pair], gathered[2 * pair + 1]], axis=1),
            preferred_element_type=f32,
        )
        for side in range(2):
            index = 2 * pair + side
            r, c = place_of(block * BLOCK + index)
            value = message[:, side * slot_count : (side + 1) * slot_count]
            valid = (lane < counts[r, c]).astype(f32)
            logistic = 1.0 / (1.0 + jnp.exp(-value))
            outgoing[index] = (value * logistic * valid).T.astype(bf16)
            slope[:, index * slot_count : (index + 1) * slot_count] = (
                valid * logistic * (1.0 + value * (1.0 - logistic))
            )
    for copy in sends(block):
        copy.start()

    @pl.when(block == pl.num_programs(0) - 1)
    def _():
        for copy in sends(block):
            copy.wait()


def bin_marks(bins):
    return [
        jnp.broadcast_to(bins[n : n + 1].astype(f32), (TILE, bins.shape[1])).astype(bf16)
        for n in range(bins.shape[0])
    ]


def backward_kernel(
    dims, scale, codes, slots, slope, coupling, gathered, bins_ref, weights, returned, *rest
):
    rows, cols, slot_count, channels, radial, neigh = dims
    own, grad = rest[:2]
    sends = rest[2:10]
    padded, full_a, full_b, total, home_grad, grads_a, grads_b, sem = rest[10:]
    width = radial * channels
    block = pl.program_id(0)
    wide = cols + 2
    leaves = rows * cols

    @pl.when(block == 0)
    def _():
        copies = [
            pltpu.make_async_copy(
                returned.at[slots[leaf // cols, leaf % cols] // leaves],
                home_grad.at[leaf],
                sem.at[leaf],
            )
            for leaf in range(leaves)
        ]
        for copy in copies:
            copy.start()
        padded[...] = jnp.zeros_like(padded)
        total[...] = jnp.zeros_like(total)
        for copy in copies:
            copy.wait()

    span = width // BLOCK

    def prepare(at, grads):
        for index in range(BLOCK):
            leaf = at * BLOCK + index
            low = index * slot_count
            first = pl.multiple_of(leaf * slot_count, slot_count)
            grads[:, low : low + slot_count] = (
                home_grad[leaf].astype(f32).T * slope[:, pl.ds(first, slot_count)]
            ).astype(bf16)

    chunks = 8
    rows_each = span // chunks

    def expand(index, chunk, grads, full):
        first = pl.multiple_of(index * span + chunk * rows_each, rows_each)
        product = jnp.dot(
            weights[pl.ds(first, rows_each), :], grads[...], preferred_element_type=f32
        ).astype(bf16)
        for leaf in range(BLOCK):
            full[leaf, pl.ds(first, rows_each), :] = product[
                :, leaf * slot_count : (leaf + 1) * slot_count
            ]

    def collect_weight(index, chunk, grads):
        low = 2 * chunk * rows_each
        first = pl.multiple_of(index * span + low, rows_each)
        total[index, :, low : low + 2 * rows_each] += lax.dot_general(
            grads[...],
            jnp.concatenate(
                [gathered[leaf, pl.ds(first, 2 * rows_each), :] for leaf in range(BLOCK)], axis=1
            ),
            (((1,), (1,)), ((), ())),
            preferred_element_type=f32,
        )

    def work(now, later):
        grads, full = now
        grads_later, full_later = later
        prepare(jnp.minimum(block + 1, pl.num_programs(0) - 1), grads_later)
        per_half = channels // TILE // 2
        bins_each = 2 * radial // chunks

        def leaf_step(index, carry):
            leaf = block * BLOCK + index
            r = leaf // cols
            c = leaf % cols
            marks = bin_marks(bins_ref[leaf])
            halves = [[] for _ in range(neigh)]
            for half in range(2):
                spots = [(half * per_half + part) * TILE for part in range(per_half)]
                values = [[jnp.zeros((TILE, slot_count), bf16)] * per_half for _ in range(neigh)]
                for quarter in range(chunks // 2):
                    chunk = half * (chunks // 2) + quarter
                    expand(index, chunk, grads_later, full_later)
                    if chunk % 2 == 0:
                        collect_weight(index, chunk // 2, grads)
                    for k in range(quarter * bins_each, (quarter + 1) * bins_each):
                        masks = [mark == jnp.bfloat16(k) for mark in marks]
                        for part, spot in enumerate(spots):
                            first = k * channels + spot
                            row = full[index, first : first + TILE, :]
                            for n in range(neigh):
                                values[n][part] = jnp.where(masks[n], row, values[n][part])
                for n in range(neigh):
                    halves[n].extend(values[n])
            for n in range(neigh):
                code = codes[r, n, c]
                sender = (r + code // 3) * wide + c + code % 3
                padded[sender] += jnp.dot(
                    jnp.concatenate(halves[n], axis=0),
                    coupling[index * neigh + n],
                    preferred_element_type=f32,
                )
            return carry

        lax.fori_loop(0, BLOCK, leaf_step, 0)

    first_set, second_set = (grads_a, full_a), (grads_b, full_b)

    @pl.when(block == 0)
    def _():
        prepare(block, grads_a)

        def first_step(index, carry):
            for chunk in range(chunks):
                expand(index, chunk, grads_a, full_a)
            return carry

        lax.fori_loop(0, BLOCK, first_step, 0)

    @pl.when(block % 2 == 0)
    def _():
        work(first_set, second_set)

    @pl.when(block % 2 == 1)
    def _():
        work(second_set, first_set)

    @pl.when(block == pl.num_programs(0) - 1)
    def _():
        for r in range(rows):
            first = (r + 1) * wide + 1
            own[r * cols : (r + 1) * cols] = padded[first : first + cols]
        for step, send in zip(STEPS, sends):
            for index, (r, c) in enumerate(rim(step, rows, cols)):
                send[index] = padded[r * wide + c].astype(send.dtype)
        per_span = span // channels
        for k in range(radial):
            low = k % per_span * channels
            grad[k * channels : (k + 1) * channels, :] = (
                total[k // per_span, :, low : low + channels].T * scale
            ).astype(grad.dtype)


def fold_kernel(dims, own, *rest):
    rows, cols = dims
    received = rest[:8]
    out, total = rest[8:]
    total[...] = own[...]
    for step, piece in zip(STEPS, received):
        for index, (r, c) in enumerate(border((-step[0], -step[1]), rows, cols)):
            total[r * cols + c] += piece[index].astype(f32)
    for leaf in range(rows * cols):
        out[leaf] = total[leaf].T.astype(bf16)


def collect_kernel(leaves, slots, arrived, out, sem):
    copies = [
        pltpu.make_async_copy(arrived.at[slots[g] // leaves], out.at[g], sem.at[g])
        for g in range(leaves)
    ]
    for copy in copies:
        copy.start()
    for copy in copies:
        copy.wait()


def shift(value, step, shape):
    gx, gy = shape
    pairs = [
        (i * gy + j, (i + step[0]) % gx * gy + (j + step[1]) % gy)
        for i in range(gx)
        for j in range(gy)
    ]
    return lax.ppermute(value, AXES, pairs)


def relay(buffer):
    return lax.all_to_all(buffer, AXES, split_axis=0, concat_axis=0, tiled=True)


def shards(
    features,
    positions,
    neighbours,
    atom_counts,
    radial_bins,
    destination,
    anchor,
    weights,
    cotangent,
):
    rows, cols, slot_count, channels = features.shape
    neigh = neighbours.shape[2]
    radial = weights.shape[0]
    leaves = rows * cols
    shape = (lax.axis_size("gx"), lax.axis_size("gy"))
    peers = shape[0] * shape[1]
    padded = (rows + 2) * (cols + 2)
    blocks = leaves // BLOCK
    tall = slot_count + POS_ROWS
    width = radial * channels
    any_dma = pltpu.SemaphoreType.DMA

    codes = neighbours.transpose(0, 2, 1)
    bins = radial_bins.reshape(leaves, neigh, slot_count)
    weight_rows = weights.reshape(width, channels)
    sizes = [len(border(step, rows, cols)) for step in STEPS]

    home, *rest = pl.pallas_call(
        functools.partial(pack_kernel, (rows, cols, slot_count)),
        out_shape=[jax.ShapeDtypeStruct((leaves, tall, channels), bf16)]
        + [jax.ShapeDtypeStruct((size, tall, channels), bf16) for size in sizes[:SIDES]]
        + [jax.ShapeDtypeStruct((peers, slot_count, channels), bf16)],
        in_specs=[smem(), smem(), vmem(), vmem(), vmem()],
        out_specs=[vmem()] * (SIDES + 1) + [hbm()],
        scratch_shapes=[any_dma((leaves,))],
        compiler_params=params(),
        name="pack",
    )(
        atom_counts,
        anchor,
        features.reshape(leaves, slot_count, channels),
        positions.transpose(0, 2, 1, 3),
        cotangent,
    )
    sends, cot_packed = rest[:SIDES], rest[SIDES]
    halos = []
    for send, step in zip(sends, STEPS):
        halos.append(shift(send, step, shape))
    low, high = halos[:2]
    for step, at in (((0, 1), cols - 1), ((0, -1), 0)):
        corners = jnp.concatenate([low[at : at + 1], high[at : at + 1]], axis=0)
        halos.append(shift(corners, step, shape))
    returned = relay(cot_packed)

    slope, coupling, gathered, packed = pl.pallas_call(
        functools.partial(forward_kernel, (rows, cols, slot_count, channels, radial, neigh)),
        grid=(blocks,),
        out_shape=[
            jax.ShapeDtypeStruct((channels, leaves * slot_count), f32),
            jax.ShapeDtypeStruct((leaves * neigh, slot_count, slot_count), bf16),
            jax.ShapeDtypeStruct((leaves, width, slot_count), bf16),
            jax.ShapeDtypeStruct((peers, slot_count, channels), bf16),
        ],
        in_specs=[smem(), smem(), smem(), hbm()] + [hbm()] * (SIDES + 2) + [vmem(), vmem()],
        out_specs=[
            pl.BlockSpec((channels, BLOCK * slot_count), lambda b: (0, b)),
            pl.BlockSpec((BLOCK * neigh, slot_count, slot_count), lambda b: (b, 0, 0)),
            pl.BlockSpec((BLOCK, width, slot_count), lambda b: (b, 0, 0)),
            hbm(),
        ],
        scratch_shapes=[
            pltpu.VMEM((padded, tall, channels), bf16),
            pltpu.VMEM((padded, channels, slot_count), bf16),
            pltpu.VMEM((channels, width), bf16),
            pltpu.VMEM((BLOCK, slot_count, channels), bf16),
            any_dma((2 * (rows + cols) + rows + 8,)),
            any_dma((BLOCK,)),
        ],
        compiler_params=params(dimension_semantics=("arbitrary",)),
        name="forward",
    )(codes, atom_counts, destination, home, *halos, bins, weight_rows)

    arrived = relay(packed)

    grad_scale = 1.0 / math.sqrt(peers * leaves * slot_count)
    own, weight_part, *grad_sends = pl.pallas_call(
        functools.partial(
            backward_kernel, (rows, cols, slot_count, channels, radial, neigh), grad_scale
        ),
        grid=(blocks,),
        out_shape=[
            jax.ShapeDtypeStruct((leaves, channels, slot_count), f32),
            jax.ShapeDtypeStruct((width, channels), bf16),
        ]
        + [jax.ShapeDtypeStruct((size, channels, slot_count), bf16) for size in sizes],
        in_specs=[
            smem(),
            smem(),
            vmem(),
            pl.BlockSpec((BLOCK * neigh, slot_count, slot_count), lambda b: (b, 0, 0)),
            pl.BlockSpec((BLOCK, width, slot_count), lambda b: (b, 0, 0)),
            vmem(),
            vmem(),
            hbm(),
        ],
        out_specs=[vmem()] * 10,
        scratch_shapes=[
            pltpu.VMEM((padded, channels, slot_count), f32),
            pltpu.VMEM((BLOCK, width, slot_count), bf16),
            pltpu.VMEM((BLOCK, width, slot_count), bf16),
            pltpu.VMEM((BLOCK, channels, width // BLOCK), f32),
            pltpu.VMEM((leaves, slot_count, channels), bf16),
            pltpu.VMEM((channels, BLOCK * slot_count), bf16),
            pltpu.VMEM((channels, BLOCK * slot_count), bf16),
            any_dma((leaves,)),
        ],
        compiler_params=params(dimension_semantics=("arbitrary",)),
        name="backward",
    )(codes, destination, slope, coupling, gathered, bins, weight_rows, returned)

    weight_pieces = relay(weight_part.reshape(peers, width // peers, channels))

    received = []
    for send, step in zip(grad_sends, STEPS):
        received.append(shift(send, step, shape))
    feature_grad = pl.pallas_call(
        functools.partial(fold_kernel, (rows, cols)),
        out_shape=jax.ShapeDtypeStruct((leaves, slot_count, channels), bf16),
        in_specs=[vmem()] * 9,
        out_specs=vmem(),
        scratch_shapes=[pltpu.VMEM((leaves, slot_count, channels), f32)],
        compiler_params=params(),
        name="fold",
    )(own, *received)

    updated = pl.pallas_call(
        functools.partial(collect_kernel, leaves),
        out_shape=jax.ShapeDtypeStruct((leaves, slot_count, channels), bf16),
        in_specs=[smem(), hbm()],
        out_specs=vmem(),
        scratch_shapes=[any_dma((leaves,))],
        compiler_params=params(),
        name="collect",
    )(anchor, arrived)

    weight_grad = jnp.sum(weight_pieces.astype(f32), axis=0)
    return updated, feature_grad.reshape(rows, cols, slot_count, channels), weight_grad


def solution(mesh):
    leaf = P("gx", "gy")
    placed = (leaf, leaf, leaf, leaf, leaf, leaf, P(AXES), P(), P(AXES))
    return jax.shard_map(
        shards,
        mesh=mesh,
        in_specs=placed,
        out_specs=(P(AXES), leaf, P(AXES)),
        check_vma=False,
    )
```

```python
import functools
import math

import jax
import jax.numpy as jnp
from jax import lax
from jax.experimental import pallas as pl
from jax.experimental.pallas import tpu as pltpu
from jax.sharding import PartitionSpec as P


AXES = ("gx", "gy")
SHARPNESS = 2.0
FAR = 9984.0
POS_ROWS = 16
BLOCK = 4
TILE = 16
VMEM_LIMIT = 60 * 1024 * 1024

f32 = jnp.float32
bf16 = jnp.bfloat16

SIDES = 4
STEPS = ((1, 0), (-1, 0), (0, 1), (0, -1), (1, 1), (1, -1), (-1, 1), (-1, -1))


def picks(step, grid, low, span):
    if step == 0:
        return list(range(low, low + span))
    return [grid[1]] if step > 0 else [grid[0]]


def border(step, rows, cols):
    return [
        (r, c)
        for r in picks(step[0], (0, rows - 1), 0, rows)
        for c in picks(step[1], (0, cols - 1), 0, cols)
    ]


def rim(step, rows, cols):
    return [
        (r, c)
        for r in picks(step[0], (0, rows + 1), 1, rows)
        for c in picks(step[1], (0, cols + 1), 1, cols)
    ]


def vmem(*_):
    return pl.BlockSpec(memory_space=pltpu.VMEM)


def hbm(*_):
    return pl.BlockSpec(memory_space=pl.ANY)


def smem(*_):
    return pl.BlockSpec(memory_space=pltpu.SMEM)


def params(**extra):
    return pltpu.CompilerParams(vmem_limit_bytes=VMEM_LIMIT, **extra)


def place_block(dims, counts, positions, r, c):
    slot_count = dims[2]
    lane = lax.broadcasted_iota(jnp.int32, (1, slot_count), 1)
    place = [positions[r, axis, c : c + 1].astype(f32) for axis in range(3)]
    place[0] = jnp.where(lane < counts[r, c], place[0], FAR)
    pad = jnp.zeros((POS_ROWS - 3, slot_count), f32)
    return jnp.concatenate(place + [pad], axis=0).astype(bf16)


def side_kernel(dims, counts, features, positions, *rest):
    rows, cols, slot_count = dims
    sends, sem = rest[:SIDES], rest[SIDES]
    copies = []
    for step, send in zip(STEPS, sends):
        for index, (r, c) in enumerate(border(step, rows, cols)):
            copies.append(
                pltpu.make_async_copy(
                    features.at[r * cols + c],
                    send.at[index, pl.ds(0, slot_count)],
                    sem.at[len(copies)],
                )
            )
    for copy in copies:
        copy.start()
    for step, send in zip(STEPS, sends):
        for index, (r, c) in enumerate(border(step, rows, cols)):
            send[index, slot_count:, :] = place_block(dims, counts, positions, r, c)
    for copy in copies:
        copy.wait()


def pack_kernel(dims, counts, slots, features, positions, cotangent, home, packed, sem):
    rows, cols, slot_count = dims
    leaves = rows * cols
    copies = [
        pltpu.make_async_copy(cotangent.at[g], packed.at[slots[g] // leaves], sem.at[g])
        for g in range(leaves)
    ]
    for copy in copies:
        copy.start()
    for r in range(rows):
        for c in range(cols):
            home[r * cols + c, slot_count:, :] = place_block(dims, counts, positions, r, c)
    home[:, :slot_count, :] = features[...]
    for copy in copies:
        copy.wait()


def forward_kernel(dims, codes, counts, slots, home, *rest):
    rows, cols, slot_count, channels, radial, neigh = dims
    halos = rest[: SIDES + 2]
    bins_ref, weights = rest[SIDES + 2 : SIDES + 4]
    slope, coupling_out, gathered, packed = rest[SIDES + 4 : SIDES + 8]
    ghost, turned, weights_t, outgoing, sem_in, sem_out = rest[SIDES + 8 :]
    block = pl.program_id(0)
    wide = cols + 2
    leaves = rows * cols

    @pl.when(block == 0)
    def _():
        copies = []
        for r in range(rows):
            copies.append((home.at[pl.ds(r * cols, cols)], ghost.at[pl.ds((r + 1) * wide + 1, cols)]))
        spots = [rim((-step[0], -step[1]), rows, cols) for step in STEPS[:SIDES]]
        spots += [[(0, c), (rows + 1, c)] for c in (0, cols + 1)]
        for spot, halo in zip(spots, halos):
            if len(spot) == cols:
                copies.append((halo, ghost.at[pl.ds(spot[0][0] * wide + spot[0][1], cols)]))
            else:
                for index, (r, c) in enumerate(spot):
                    copies.append((halo.at[index], ghost.at[r * wide + c]))
        copies = [
            pltpu.make_async_copy(source, target, sem_in.at[index])
            for index, (source, target) in enumerate(copies)
        ]
        for copy in copies:
            copy.start()
        for k in range(radial):
            weights_t[:, k * channels : (k + 1) * channels] = weights[
                k * channels : (k + 1) * channels, :
            ].T
        for copy in copies:
            copy.wait()

        def turn(leaf, carry):
            turned[leaf] = ghost[leaf, pl.ds(0, slot_count), :].T
            return carry

        lax.fori_loop(0, (rows + 2) * wide, turn, 0, unroll=4)

    row_index = lax.broadcasted_iota(jnp.int32, (slot_count, slot_count), 0)
    col_index = lax.broadcasted_iota(jnp.int32, (slot_count, slot_count), 1)
    lane = lax.broadcasted_iota(jnp.int32, (channels, slot_count), 1)

    def place_of(leaf):
        return leaf // cols, leaf % cols

    def build(index):
        leaf = block * BLOCK + index
        r, c = place_of(leaf)
        own = (r + 1) * wide + c + 1
        place = ghost[own, pl.ds(slot_count, POS_ROWS), :].astype(f32)
        columns = place[:8].T
        receiver = [
            jnp.broadcast_to(columns[:, axis : axis + 1], (slot_count, slot_count))
            for axis in range(3)
        ]
        bins = bins_ref[leaf]
        tiles = []
        for n in range(neigh):
            code = codes[r, n, c]
            row_off = code // 3
            col_off = code % 3
            sender = (r + row_off) * wide + c + col_off
            remote = ghost[sender, pl.ds(slot_count, POS_ROWS), :].astype(f32)
            delta_x = (remote[0:1] + (row_off - 1).astype(f32)) - receiver[0]
            delta_y = (remote[1:2] + (col_off - 1).astype(f32)) - receiver[1]
            delta_z = remote[2:3] - receiver[2]
            distance = delta_x * delta_x + delta_y * delta_y + delta_z * delta_z
            coupling = jnp.exp(-SHARPNESS * distance)
            if n == 0:
                coupling = jnp.where(row_index == col_index, 0.0, coupling)
            coupling = coupling.astype(bf16)
            coupling_out[index * neigh + n] = coupling
            tiles.append(
                lax.dot_general(
                    turned[sender],
                    coupling,
                    (((1,), (1,)), ((), ())),
                    preferred_element_type=f32,
                )
            )
        merged = []
        for n in range(neigh):
            total = tiles[n]
            for m in range(n):
                same = jnp.broadcast_to(bins[m : m + 1] == bins[n : n + 1], total.shape)
                total = total + jnp.where(same, tiles[m], 0.0)
            merged.append(total.astype(bf16))
        marks = bin_marks(bins)
        for k in range(radial):
            masks = [mark == jnp.bfloat16(k) for mark in marks]
            for part in range(channels // TILE):
                value = jnp.zeros((TILE, slot_count), bf16)
                for n in range(neigh):
                    value = jnp.where(
                        masks[n], merged[n][part * TILE : (part + 1) * TILE], value
                    )
                first = k * channels + part * TILE
                gathered[index, first : first + TILE, :] = value

    def sends(at):
        copies = []
        for index in range(BLOCK):
            r, c = place_of(at * BLOCK + index)
            copies.append(
                pltpu.make_async_copy(
                    outgoing.at[index], packed.at[slots[r, c] // leaves], sem_out.at[index]
                )
            )
        return copies

    @pl.when(block > 0)
    def _():
        for copy in sends(block - 1):
            copy.wait()

    for pair in range(BLOCK // 2):
        for index in (2 * pair, 2 * pair + 1):
            build(index)
        message = jnp.dot(
            weights_t[...],
            jnp.concatenate([gathered[2 * pair], gathered[2 * pair + 1]], axis=1),
            preferred_element_type=f32,
        )
        for side in range(2):
            index = 2 * pair + side
            r, c = place_of(block * BLOCK + index)
            value = message[:, side * slot_count : (side + 1) * slot_count]
            valid = (lane < counts[r, c]).astype(f32)
            logistic = 1.0 / (1.0 + jnp.exp(-value))
            outgoing[index] = (value * logistic * valid).T.astype(bf16)
            slope[:, index * slot_count : (index + 1) * slot_count] = (
                valid * logistic * (1.0 + value * (1.0 - logistic))
            )
    for copy in sends(block):
        copy.start()

    @pl.when(block == pl.num_programs(0) - 1)
    def _():
        for copy in sends(block):
            copy.wait()


def bin_marks(bins):
    return [
        jnp.broadcast_to(bins[n : n + 1].astype(f32), (TILE, bins.shape[1])).astype(bf16)
        for n in range(bins.shape[0])
    ]


def backward_kernel(
    dims, scale, codes, slots, slope, coupling, gathered, bins_ref, weights, returned, *rest
):
    rows, cols, slot_count, channels, radial, neigh = dims
    own, grad = rest[:2]
    sends = rest[2:10]
    padded, full_a, full_b, total, home_grad, grads_a, grads_b, sem = rest[10:]
    width = radial * channels
    block = pl.program_id(0)
    wide = cols + 2
    leaves = rows * cols

    @pl.when(block == 0)
    def _():
        copies = [
            pltpu.make_async_copy(
                returned.at[slots[leaf // cols, leaf % cols] // leaves],
                home_grad.at[leaf],
                sem.at[leaf],
            )
            for leaf in range(leaves)
        ]
        for copy in copies:
            copy.start()
        padded[...] = jnp.zeros_like(padded)
        total[...] = jnp.zeros_like(total)
        for copy in copies:
            copy.wait()

    span = width // BLOCK

    def prepare(at, grads):
        for index in range(BLOCK):
            leaf = at * BLOCK + index
            low = index * slot_count
            first = pl.multiple_of(leaf * slot_count, slot_count)
            grads[:, low : low + slot_count] = (
                home_grad[leaf].astype(f32).T * slope[:, pl.ds(first, slot_count)]
            ).astype(bf16)

    chunks = 8
    rows_each = span // chunks

    def expand(index, chunk, grads, full):
        first = pl.multiple_of(index * span + chunk * rows_each, rows_each)
        product = jnp.dot(
            weights[pl.ds(first, rows_each), :], grads[...], preferred_element_type=f32
        ).astype(bf16)
        for leaf in range(BLOCK):
            full[leaf, pl.ds(first, rows_each), :] = product[
                :, leaf * slot_count : (leaf + 1) * slot_count
            ]

    def collect_weight(index, chunk, grads):
        low = 2 * chunk * rows_each
        first = pl.multiple_of(index * span + low, rows_each)
        total[index, :, low : low + 2 * rows_each] += lax.dot_general(
            grads[...],
            jnp.concatenate(
                [gathered[leaf, pl.ds(first, 2 * rows_each), :] for leaf in range(BLOCK)], axis=1
            ),
            (((1,), (1,)), ((), ())),
            preferred_element_type=f32,
        )

    def work(now, later):
        grads, full = now
        grads_later, full_later = later
        prepare(jnp.minimum(block + 1, pl.num_programs(0) - 1), grads_later)
        per_half = channels // TILE // 2
        bins_each = 2 * radial // chunks

        def leaf_step(index, carry):
            leaf = block * BLOCK + index
            r = leaf // cols
            c = leaf % cols
            marks = bin_marks(bins_ref[leaf])
            halves = [[] for _ in range(neigh)]
            for half in range(2):
                spots = [(half * per_half + part) * TILE for part in range(per_half)]
                values = [[jnp.zeros((TILE, slot_count), bf16)] * per_half for _ in range(neigh)]
                for quarter in range(chunks // 2):
                    chunk = half * (chunks // 2) + quarter
                    expand(index, chunk, grads_later, full_later)
                    if chunk % 2 == 0:
                        collect_weight(index, chunk // 2, grads)
                    for k in range(quarter * bins_each, (quarter + 1) * bins_each):
                        masks = [mark == jnp.bfloat16(k) for mark in marks]
                        for part, spot in enumerate(spots):
                            first = k * channels + spot
                            row = full[index, first : first + TILE, :]
                            for n in range(neigh):
                                values[n][part] = jnp.where(masks[n], row, values[n][part])
                for n in range(neigh):
                    halves[n].extend(values[n])
            for n in range(neigh):
                code = codes[r, n, c]
                sender = (r + code // 3) * wide + c + code % 3
                padded[sender] += jnp.dot(
                    jnp.concatenate(halves[n], axis=0),
                    coupling[index * neigh + n],
                    preferred_element_type=f32,
                )
            return carry

        lax.fori_loop(0, BLOCK, leaf_step, 0)

    first_set, second_set = (grads_a, full_a), (grads_b, full_b)

    @pl.when(block == 0)
    def _():
        prepare(block, grads_a)

        def first_step(index, carry):
            for chunk in range(chunks):
                expand(index, chunk, grads_a, full_a)
            return carry

        lax.fori_loop(0, BLOCK, first_step, 0)

    @pl.when(block % 2 == 0)
    def _():
        work(first_set, second_set)

    @pl.when(block % 2 == 1)
    def _():
        work(second_set, first_set)

    @pl.when(block == pl.num_programs(0) - 1)
    def _():
        for r in range(rows):
            first = (r + 1) * wide + 1
            own[r * cols : (r + 1) * cols] = padded[first : first + cols]
        for step, send in zip(STEPS, sends):
            for index, (r, c) in enumerate(rim(step, rows, cols)):
                send[index] = padded[r * wide + c].astype(send.dtype)
        per_span = span // channels
        for k in range(radial):
            low = k % per_span * channels
            grad[k * channels : (k + 1) * channels, :] = (
                total[k // per_span, :, low : low + channels].T * scale
            ).astype(grad.dtype)


def corner_leaves(rows, cols):
    return [(r, c) for r in (0, rows - 1) for c in (0, cols - 1)]


def fold_kernel(dims, own, *rest):
    rows, cols = dims
    received = rest[:SIDES]
    out, corners, total = rest[SIDES:]
    total[...] = own[...]
    for step, piece in zip(STEPS, received):
        for index, (r, c) in enumerate(border((-step[0], -step[1]), rows, cols)):
            total[r * cols + c] += piece[index].astype(f32)
    for leaf in range(rows * cols):
        out[leaf] = total[leaf].T.astype(bf16)
    for index, (r, c) in enumerate(corner_leaves(rows, cols)):
        corners[index] = total[r * cols + c]


def corner_kernel(dims, folded, corners, *rest):
    rows, cols = dims
    received = rest[: len(STEPS) - SIDES]
    out, ready, sem = rest[len(STEPS) - SIDES :]
    places = corner_leaves(rows, cols)
    copies = []
    for step, piece in zip(STEPS[SIDES:], received):
        place = border((-step[0], -step[1]), rows, cols)[0]
        index = places.index(place)
        ready[index] = (corners[index] + piece[0].astype(f32)).T.astype(bf16)
        copies.append(
            pltpu.make_async_copy(
                ready.at[index], out.at[place[0] * cols + place[1]], sem.at[index]
            )
        )
    for copy in copies:
        copy.start()
    for copy in copies:
        copy.wait()


def collect_kernel(leaves, slots, arrived, out, sem):
    copies = [
        pltpu.make_async_copy(arrived.at[slots[g] // leaves], out.at[g], sem.at[g])
        for g in range(leaves)
    ]
    for copy in copies:
        copy.start()
    for copy in copies:
        copy.wait()


def shift(value, step, shape):
    gx, gy = shape
    pairs = [
        (i * gy + j, (i + step[0]) % gx * gy + (j + step[1]) % gy)
        for i in range(gx)
        for j in range(gy)
    ]
    return lax.ppermute(value, AXES, pairs)


def relay(buffer):
    return lax.all_to_all(buffer, AXES, split_axis=0, concat_axis=0, tiled=True)


def shards(
    features,
    positions,
    neighbours,
    atom_counts,
    radial_bins,
    destination,
    anchor,
    weights,
    cotangent,
):
    rows, cols, slot_count, channels = features.shape
    neigh = neighbours.shape[2]
    radial = weights.shape[0]
    leaves = rows * cols
    shape = (lax.axis_size("gx"), lax.axis_size("gy"))
    peers = shape[0] * shape[1]
    padded = (rows + 2) * (cols + 2)
    blocks = leaves // BLOCK
    tall = slot_count + POS_ROWS
    width = radial * channels
    any_dma = pltpu.SemaphoreType.DMA

    codes = neighbours.transpose(0, 2, 1)
    bins = radial_bins.reshape(leaves, neigh, slot_count)
    weight_rows = weights.reshape(width, channels)
    sizes = [len(border(step, rows, cols)) for step in STEPS]

    flat = features.reshape(leaves, slot_count, channels)
    places = positions.transpose(0, 2, 1, 3)
    sends = pl.pallas_call(
        functools.partial(side_kernel, (rows, cols, slot_count)),
        out_shape=[jax.ShapeDtypeStruct((size, tall, channels), bf16) for size in sizes[:SIDES]],
        in_specs=[smem(), hbm(), vmem()],
        out_specs=[vmem()] * SIDES,
        scratch_shapes=[any_dma((sum(sizes[:SIDES]),))],
        compiler_params=params(),
        name="pack_sides",
    )(atom_counts, flat, places)
    home, cot_packed = pl.pallas_call(
        functools.partial(pack_kernel, (rows, cols, slot_count)),
        out_shape=[
            jax.ShapeDtypeStruct((leaves, tall, channels), bf16),
            jax.ShapeDtypeStruct((peers, slot_count, channels), bf16),
        ],
        in_specs=[smem(), smem(), vmem(), vmem(), vmem()],
        out_specs=[vmem(), hbm()],
        scratch_shapes=[any_dma((leaves,))],
        compiler_params=params(),
        name="pack_rest",
    )(atom_counts, anchor, flat, places, cotangent)
    halos = []
    for send, step in zip(sends, STEPS):
        halos.append(shift(send, step, shape))
    low, high = halos[:2]
    for step, at in (((0, 1), cols - 1), ((0, -1), 0)):
        corners = jnp.concatenate([low[at : at + 1], high[at : at + 1]], axis=0)
        halos.append(shift(corners, step, shape))
    returned = relay(cot_packed)

    slope, coupling, gathered, packed = pl.pallas_call(
        functools.partial(forward_kernel, (rows, cols, slot_count, channels, radial, neigh)),
        grid=(blocks,),
        out_shape=[
            jax.ShapeDtypeStruct((channels, leaves * slot_count), f32),
            jax.ShapeDtypeStruct((leaves * neigh, slot_count, slot_count), bf16),
            jax.ShapeDtypeStruct((leaves, width, slot_count), bf16),
            jax.ShapeDtypeStruct((peers, slot_count, channels), bf16),
        ],
        in_specs=[smem(), smem(), smem(), hbm()] + [hbm()] * (SIDES + 2) + [vmem(), vmem()],
        out_specs=[
            pl.BlockSpec((channels, BLOCK * slot_count), lambda b: (0, b)),
            pl.BlockSpec((BLOCK * neigh, slot_count, slot_count), lambda b: (b, 0, 0)),
            pl.BlockSpec((BLOCK, width, slot_count), lambda b: (b, 0, 0)),
            hbm(),
        ],
        scratch_shapes=[
            pltpu.VMEM((padded, tall, channels), bf16),
            pltpu.VMEM((padded, channels, slot_count), bf16),
            pltpu.VMEM((channels, width), bf16),
            pltpu.VMEM((BLOCK, slot_count, channels), bf16),
            any_dma((2 * (rows + cols) + rows + 8,)),
            any_dma((BLOCK,)),
        ],
        compiler_params=params(dimension_semantics=("arbitrary",)),
        name="forward",
    )(codes, atom_counts, destination, home, *halos, bins, weight_rows)

    arrived = relay(packed)

    grad_scale = 1.0 / math.sqrt(peers * leaves * slot_count)
    own, weight_part, *grad_sends = pl.pallas_call(
        functools.partial(
            backward_kernel, (rows, cols, slot_count, channels, radial, neigh), grad_scale
        ),
        grid=(blocks,),
        out_shape=[
            jax.ShapeDtypeStruct((leaves, channels, slot_count), f32),
            jax.ShapeDtypeStruct((width, channels), bf16),
        ]
        + [jax.ShapeDtypeStruct((size, channels, slot_count), bf16) for size in sizes],
        in_specs=[
            smem(),
            smem(),
            vmem(),
            pl.BlockSpec((BLOCK * neigh, slot_count, slot_count), lambda b: (b, 0, 0)),
            pl.BlockSpec((BLOCK, width, slot_count), lambda b: (b, 0, 0)),
            vmem(),
            vmem(),
            hbm(),
        ],
        out_specs=[vmem()] * 10,
        scratch_shapes=[
            pltpu.VMEM((padded, channels, slot_count), f32),
            pltpu.VMEM((BLOCK, width, slot_count), bf16),
            pltpu.VMEM((BLOCK, width, slot_count), bf16),
            pltpu.VMEM((BLOCK, channels, width // BLOCK), f32),
            pltpu.VMEM((leaves, slot_count, channels), bf16),
            pltpu.VMEM((channels, BLOCK * slot_count), bf16),
            pltpu.VMEM((channels, BLOCK * slot_count), bf16),
            any_dma((leaves,)),
        ],
        compiler_params=params(dimension_semantics=("arbitrary",)),
        name="backward",
    )(codes, destination, slope, coupling, gathered, bins, weight_rows, returned)

    weight_pieces = relay(weight_part.reshape(peers, width // peers, channels))

    received = []
    for send, step in zip(grad_sends, STEPS):
        received.append(shift(send, step, shape))
    folded, corners = pl.pallas_call(
        functools.partial(fold_kernel, (rows, cols)),
        out_shape=[
            jax.ShapeDtypeStruct((leaves, slot_count, channels), bf16),
            jax.ShapeDtypeStruct((len(STEPS) - SIDES, channels, slot_count), f32),
        ],
        in_specs=[vmem()] * (SIDES + 1),
        out_specs=[vmem(), vmem()],
        scratch_shapes=[pltpu.VMEM((leaves, channels, slot_count), f32)],
        compiler_params=params(),
        name="fold_sides",
    )(own, *received[:SIDES])
    feature_grad = pl.pallas_call(
        functools.partial(corner_kernel, (rows, cols)),
        out_shape=jax.ShapeDtypeStruct((leaves, slot_count, channels), bf16),
        in_specs=[hbm()] + [vmem()] * (len(STEPS) - SIDES + 1),
        out_specs=hbm(),
        scratch_shapes=[
            pltpu.VMEM((len(STEPS) - SIDES, slot_count, channels), bf16),
            any_dma((len(STEPS) - SIDES,)),
        ],
        input_output_aliases={0: 0},
        compiler_params=params(),
        name="fold_corners",
    )(folded, corners, *received[SIDES:])

    updated = pl.pallas_call(
        functools.partial(collect_kernel, leaves),
        out_shape=jax.ShapeDtypeStruct((leaves, slot_count, channels), bf16),
        in_specs=[smem(), hbm()],
        out_specs=vmem(),
        scratch_shapes=[any_dma((leaves,))],
        compiler_params=params(),
        name="collect",
    )(anchor, arrived)

    weight_grad = jnp.sum(weight_pieces.astype(f32), axis=0)
    return updated, feature_grad.reshape(rows, cols, slot_count, channels), weight_grad


def solution(mesh):
    leaf = P("gx", "gy")
    placed = (leaf, leaf, leaf, leaf, leaf, leaf, P(AXES), P(), P(AXES))
    return jax.shard_map(
        shards,
        mesh=mesh,
        in_specs=placed,
        out_specs=(P(AXES), leaf, P(AXES)),
        check_vma=False,
    )
```
